256 devices in a mesh: row: 64 (over z, y, core), col: 4 (over x).
Axes of the slice: x: 4, y: 4, z: 8, core: 2. Of those that a mesh axis runs over, the one named last changes fastest.
Arguments:
- blocks: bfloat16 [4096, 12, 128, 128], P('row'), may hold values from -0.15625 to 0.15625
- col_index: int32 [4096, 12], P('row'), may hold values from -8 to 4103, as said below
- live_slots: int32 [4096], P('row'), may hold values from 3 to 12, as said below
- vectors: bfloat16 [256, 524288], P('col', 'row'), may hold values from -6 to 6
- center: float32 [1], replicated, may hold values from -0.4 to 0.4
- halfwidth: float32 [1], replicated, may hold values from 0.8 to 1.6
Outputs:
- ortho_basis: float32 [256, 524288], P('col', 'row')
- triangle: float32 [256, 256], replicated
The draws below stay inside these ranges and needn't reach their ends.
Inputs may be any that keep to these rules, and one draw needn't show every extreme that they name: col_index[i, k] - i lies in -8 .. 8 and is different for every k of a row; slot 0 is i, slot 1 is i + 8, slot 2 is i - 8. `live_slots`: slots 0, 1 and 2 are live in every row; the counts of one index of row lie within one of a level shared by that index (block rows 0 and 1 excepted), so whole devices are busy or light.
All inputs are finite; a program needn't handle non-finite values.
Results may differ from the reference program's by a relative error of at most 0.0042.
Values may be sent and summed in bfloat16 or wider, within the bound.
No kernel may reach another device: no remote copies, remote signals or barrier semaphores. Data moves between devices by JAX's collectives and lax.ppermute only.
A program may use at most 128 MiB of HBM per device.

```python
import jax
import jax.numpy as jnp
from jax import lax

BLOCK = 128
NV = 256
K = 12
W = 8
BR_DEV = 64
NBR = 4096
ORDER = 524288


def draw_col_index(key, part):
    row_ids = jnp.arange(NBR, dtype=jnp.int32)
    offsets_pool = jnp.concatenate([jnp.arange(-W + 1, 0, dtype=jnp.int32), jnp.arange(1, W, dtype=jnp.int32)])
    scores = jax.random.randint(jax.random.fold_in(key, 11), (NBR, 2 * W - 2), 0, 1 << 20) * (2 * W) + jnp.arange(2 * W - 2, dtype=jnp.int32)[None, :]
    ranking = jnp.argsort(scores, axis=1, stable=True)
    chosen = offsets_pool[ranking[:, :K - 3]]
    fixed_part = jnp.stack([jnp.zeros((NBR,), jnp.int32), jnp.full((NBR,), W, jnp.int32), jnp.full((NBR,), -W, jnp.int32)], axis=1)
    offsets_all = jnp.concatenate([fixed_part, chosen.astype(jnp.int32)], axis=1)
    return (row_ids[:, None] + offsets_all).astype(jnp.int32)


def draw_live_slots(key, part):
    groups = NBR // BR_DEV
    device_level = jax.random.randint(jax.random.fold_in(key, 21), (groups,), 3, K + 1)
    jitter = jax.random.randint(jax.random.fold_in(key, 22), (NBR,), -1, 2)
    counts = jnp.clip(jnp.repeat(device_level, BR_DEV) + jitter, 3, K)
    counts = counts.at[0].set(K).at[1].set(3)
    return counts.astype(jnp.int32)


def shard_levels(key, dims, pieces, smallest, high):
    level, own = 1.0, jax.random.fold_in(key, 6)
    for position, shards_of in pieces:
        draws = jnp.exp(jax.random.uniform(jax.random.fold_in(own, position), (shards_of,), jnp.float32, smallest / len(pieces), high / len(pieces)))
        level = level * jnp.repeat(draws, dims[position] // shards_of).reshape([-1 if axis == position else 1 for axis in range(len(dims))])
    return level


def noise(own_key, shape, spread, most, shards=(), held_as=jnp.bfloat16):
    factor_of = shard_levels(own_key, shape, shards, -0.22, 0.18) if shards else 1.0
    drawn = jax.random.normal(own_key, shape, jnp.float32) * spread * factor_of
    return jnp.minimum(jnp.maximum(drawn, -most), most).astype(held_as)


def setup_inputs(seed: int = 0) -> dict:
    arg_keys = jax.random.split(jax.random.key(seed), 7)
    return {
        "blocks": noise(arg_keys[0], (NBR, K, BLOCK, BLOCK), (BLOCK * K) ** -0.5, 0.15625, ((0, 64),)),
        "col_index": draw_col_index(jax.random.fold_in(arg_keys[6], 71), 0),
        "live_slots": draw_live_slots(jax.random.fold_in(arg_keys[6], 71), 0),
        "vectors": noise(arg_keys[3], (NV, ORDER), 1.0, 6.0, ((0, 4), (1, 64))),
        "center": jnp.clip(jax.random.uniform(arg_keys[4], (1,), jnp.float32, -0.4, 0.4), -0.4, 0.4),
        "halfwidth": jnp.clip(jax.random.uniform(arg_keys[5], (1,), jnp.float32, 0.8, 1.6), 0.8, 1.6),
    }


def apply_blocks(blocks, col_index, live_slots, vectors_in):
    extended = jnp.pad(vectors_in, ((0, 0), (W * BLOCK, W * BLOCK))).reshape(NV, NBR + 2 * W, BLOCK)
    groups = NBR // BR_DEV
    slot_live = jnp.arange(K, dtype=jnp.int32)[None, :] < live_slots[:, None]

    def group_product(packed):
        group_blocks, group_index, group_live = packed
        picked = jnp.take(extended, group_index.reshape(-1), axis=1).reshape(NV, BR_DEV, K, BLOCK)
        picked = jnp.where(group_live[None, :, :, None], picked.astype(jnp.float32), jnp.float32(0.0))
        return jnp.einsum('rkab,vrkb->vra', group_blocks.astype(jnp.float32), picked)
    products = lax.map(group_product, (blocks.reshape(groups, BR_DEV, K, BLOCK, BLOCK), (col_index + W).astype(jnp.int32).reshape(groups, BR_DEV, K), slot_live.reshape(groups, BR_DEV, K)))
    return jnp.transpose(products, (1, 0, 2, 3)).reshape(NV, ORDER)

def reference(blocks, col_index, live_slots, vectors, center, halfwidth):
    shift_value = center[0]
    scale_value = halfwidth[0]
    plain = vectors.astype(jnp.float32)
    first_step = ((apply_blocks(blocks, col_index, live_slots, vectors) - shift_value * plain) / scale_value).astype(jnp.bfloat16)
    second = apply_blocks(blocks, col_index, live_slots, first_step)
    filtered = (2.0 * (second - shift_value * first_step.astype(jnp.float32)) / scale_value - plain).astype(jnp.bfloat16)
    gram_matrix = lax.dot_general(filtered.astype(jnp.float32), filtered.astype(jnp.float32), (((1,), (1,)), ((), ())), preferred_element_type=jnp.float32) / ORDER
    factor = jnp.linalg.cholesky(gram_matrix)
    identity = jnp.eye(NV, dtype=gram_matrix.dtype)
    inverse = lax.linalg.triangular_solve(factor, identity, left_side=True, lower=True)
    ortho_basis = jnp.dot(inverse, filtered.astype(gram_matrix.dtype), precision=lax.Precision.HIGHEST)
    return (ortho_basis, factor.T)
```

```python
import jax
import jax.numpy as jnp
from jax import lax
from jax.experimental import pallas as pl
from jax.experimental.pallas import tpu as pltpu
from jax.sharding import PartitionSpec as P

W = 8
LANE = 128

NT = (((1,), (1,)), ((), ()))
ANY = pl.BlockSpec(memory_space=pl.ANY)
SMEM = pl.BlockSpec(memory_space=pltpu.SMEM)
VMEM = pl.BlockSpec(memory_space=pltpu.VMEM)
HIGHEST = lax.Precision.HIGHEST


def lanes(block, count=1):
    return pl.ds(pl.multiple_of(block * LANE, LANE), count * LANE)


def row_product(col_ref, live_ref, first_block, ext, blk, row, slot_row, zero_block):
    slots = blk.shape[1]
    live = live_ref[row]
    parts = []
    for k in range(slots):
        at = jnp.where(k < live, col_ref[row, k] - first_block, zero_block)
        parts.append(ext[:, lanes(at)])
    picked = jnp.concatenate(parts, axis=1)
    wide = jnp.concatenate([blk[slot_row, k] for k in range(slots)], axis=1)
    return lax.dot_general(wide, picked, NT, preferred_element_type=jnp.float32).T


def apply_call(name, second, block_rows, groups, per_group, row_of, piece_at, scal, col_index,
               live_slots, blocks, pieces, plain, outs, out_of, tail):
    width, _, slots = pieces[0].shape[0], None, blocks.shape[1]
    total = block_rows + 2 * W
    n_pieces = len(pieces)

    def kernel(*refs):
        scal_ref, col_ref, live_ref, blk_hbm = refs[:4]
        piece_refs = refs[4:4 + n_pieces]
        plain_ref = refs[4 + n_pieces] if second else None
        base = 4 + n_pieces + (1 if second else 0)
        out_refs = refs[base:base + len(outs)]
        ext, blk, stage, psem, bsem, osem = refs[base + len(outs):base + len(outs) + 6]
        plain_v = refs[-1] if second else None
        loads = [
            pltpu.make_async_copy(
                src, ext.at[:, pl.ds(at * LANE, src.shape[1])], psem.at[i])
            for i, (src, at) in enumerate(zip(piece_refs, piece_at))
        ]
        if second:
            loads.append(pltpu.make_async_copy(plain_ref, plain_v, psem.at[n_pieces]))
        for load in loads:
            load.start()

        def block_load(g):
            return pltpu.make_async_copy(
                blk_hbm.at[pl.ds(row_of(g), per_group)],
                blk.at[pl.ds(g * per_group, per_group)], bsem.at[g])

        for g in range(groups):
            block_load(g).start()
        ext[:, total * LANE:(total + 1) * LANE] = jnp.zeros((width, LANE), jnp.bfloat16)
        first_block = lax.axis_index("row") * block_rows - W
        shift = scal_ref[0]
        scale = scal_ref[1]
        for load in loads:
            load.wait()

        def store(g, i):
            at, offset = out_of(i)
            span = per_group
            return pltpu.make_async_copy(
                stage.at[g], out_refs[at].at[:, pl.ds(offset * LANE, span * LANE)], osem.at[g])

        def group(g, carry):
            block_load(g).wait()
            for r in range(per_group):
                row = row_of(g) + r
                acc = row_product(col_ref, live_ref, first_block, ext, blk, row,
                                  g * per_group + r, total)
                own = ext[:, lanes(row + W)].astype(jnp.float32)
                value = (acc - shift * own) * scale
                if second:
                    value = 2.0 * value - plain_v[:, lanes(row)].astype(jnp.float32)
                stage[g, :, r * LANE:(r + 1) * LANE] = value.astype(jnp.bfloat16)
            for i in range(groups):
                @pl.when(g == i)
                def _(i=i):
                    store(i, i).start()
            return carry

        lax.fori_loop(0, groups, group, 0)
        for i in range(groups):
            store(i, i).wait()

    scratch = [
        pltpu.VMEM((width, (total + 1) * LANE), jnp.bfloat16),
        pltpu.VMEM((groups * per_group, slots, LANE, LANE), jnp.bfloat16),
        pltpu.VMEM((groups, width, per_group * LANE), jnp.bfloat16),
        pltpu.SemaphoreType.DMA((n_pieces + 1,)),
        pltpu.SemaphoreType.DMA((groups,)),
        pltpu.SemaphoreType.DMA((groups,)),
    ]
    args = [scal, col_index, live_slots, blocks, *pieces]
    specs = [SMEM, SMEM, SMEM, ANY] + [ANY] * n_pieces
    if second:
        args.append(plain)
        specs.append(ANY)
        scratch.append(pltpu.VMEM(plain.shape, jnp.bfloat16))
    return pl.pallas_call(
        kernel, name=name, in_specs=specs, out_specs=[ANY] * len(outs), scratch_shapes=scratch,
        out_shape=[jax.ShapeDtypeStruct((width, n * LANE), jnp.bfloat16) for n in outs],
    )(*args)


def gram_call(mine, got, order_all, vectors_all):
    local, n_pieces = mine[0].shape[0], len(mine)
    widths = [m.shape[1] for m in mine]
    width = sum(widths)
    groups = vectors_all // local
    half = vectors_all // 2
    arrays = [a for m, g in zip(mine, got) for a in (m, *g)]

    def kernel(*refs):
        srcs = refs[:len(arrays)]
        field_out, keep, send, field, sem, osem = refs[len(arrays):]
        col = lax.axis_index("col")
        loads, start = [], 0
        for p in range(n_pieces):
            for s in range(groups):
                i = p * groups + s
                to = lax.rem(col - s + groups, groups) * local
                loads.append(pltpu.make_async_copy(
                    srcs[i],
                    field.at[pl.ds(pl.multiple_of(to, local), local), pl.ds(start, widths[p])],
                    sem.at[i]))
            start += widths[p]
        for load in loads:
            load.start()
        for load in loads:
            load.wait()
        out = pltpu.make_async_copy(field, field_out, osem)
        out.start()
        f = field[...]
        g = lax.dot_general(f, f, NT, preferred_element_type=jnp.float32) * (1.0 / order_all)
        core = lax.rem(lax.axis_index("row"), 2)
        quarter = half // 2

        def put(low, high):
            low[:half, :] = g[:half, :half]
            low[half:, :] = g[half:half + quarter, :half]
            high[:half, :] = g[half:, half:]
            high[half:, :] = g[half + quarter:, :half]

        @pl.when(core == 0)
        def _():
            put(keep, send)

        @pl.when(core == 1)
        def _():
            put(send, keep)

        out.wait()

    packed = jax.ShapeDtypeStruct((half + half // 2, half), jnp.float32)
    return pl.pallas_call(
        kernel, name="gram", in_specs=[ANY] * len(arrays), out_specs=[ANY, VMEM, VMEM],
        scratch_shapes=[pltpu.VMEM((vectors_all, width), jnp.bfloat16),
                        pltpu.SemaphoreType.DMA((len(arrays),)), pltpu.SemaphoreType.DMA],
        out_shape=[jax.ShapeDtypeStruct((vectors_all, width), jnp.bfloat16), packed, packed],
    )(*arrays)


def split_call(keep, other, y_of, parts):
    rows = keep.shape[0] // parts

    def kernel(a, b, *outs):
        y = y_of()
        for s in range(parts):
            at = pl.ds(pl.multiple_of(lax.rem(y + s, parts) * rows, 8), rows)
            outs[s][...] = a[at, :] + b[at, :]

    shape = jax.ShapeDtypeStruct((rows, keep.shape[1]), jnp.float32)
    return pl.pallas_call(kernel, name="split", in_specs=[VMEM] * 2, out_specs=[VMEM] * parts,
                          out_shape=[shape] * parts)(keep, other)


def merge_call(pieces, y_of):
    parts, (rows, width) = len(pieces), pieces[0].shape

    def kernel(*refs):
        out = refs[-1]
        y = y_of()
        for s in range(parts):
            at = pl.ds(pl.multiple_of(lax.rem(y - s + parts, parts) * rows, 8), rows)
            out[at, :] = refs[s][...]

    return pl.pallas_call(kernel, name="merge", in_specs=[VMEM] * parts, out_specs=VMEM,
                          out_shape=jax.ShapeDtypeStruct((rows * parts, width), jnp.float32))(*pieces)


def eliminate(a):
    n = a.shape[0]
    tile = 8
    lane = lax.broadcasted_iota(jnp.int32, (tile, n), 1)
    sub = lax.broadcasted_iota(jnp.int32, (tile, n), 0)
    count = n // tile
    rows = [a[i * tile:(i + 1) * tile, :] for i in range(count)]
    inv = [jnp.where(lane == sub + i * tile, 1.0, 0.0).astype(jnp.float32) for i in range(count)]
    upper, lower = [None] * count, [None] * count

    def spread(x, r):
        return jnp.broadcast_to(x[r:r + 1, :], (tile, n))

    def column(x, c):
        return jnp.broadcast_to(x[:, c:c + 1], (tile, n))

    for g in range(count):
        norm = jnp.zeros((tile, n), jnp.float32)
        for j in range(0, tile, 2):
            c = g * tile + j
            x, m = rows[g], inv[g]
            col0, col1 = column(x, c), column(x, c + 1)
            a0, b, d = spread(col0, j), spread(col0, j + 1), spread(col1, j + 1)
            ra = 1.0 / a0
            t = b * ra
            e = d - b * t
            re = 1.0 / e
            norm = jnp.where(sub == j, a0, jnp.where(sub == j + 1, e, norm))
            row0, m0 = spread(x, j), spread(m, j)
            row1, m1 = spread(x, j + 1) - t * row0, spread(m, j + 1) - t * m0
            for i in range(g, count):
                p0, p1 = (col0, col1) if i == g else (column(rows[i], c), column(rows[i], c + 1))
                f0 = p0 * ra
                f1 = (p1 - t * p0) * re
                if i == g:
                    f0 = jnp.where(sub > j, f0, 0.0)
                    f1 = jnp.where(sub > j + 1, f1, 0.0)
                rows[i] = rows[i] - (f0 * row0 + f1 * row1)
                inv[i] = inv[i] - (f0 * m0 + f1 * m1)
        r = lax.rsqrt(norm)
        upper[g] = jnp.where(lane >= sub + g * tile, rows[g] * r, 0.0)
        lower[g] = inv[g] * r
    return jnp.concatenate(upper, axis=0), jnp.concatenate(lower, axis=0)


def factor_call(own, other):
    rows, half = own.shape
    quarter = half // 2
    n = 2 * half

    def kernel(x_ref, y_ref, tri, low, work):
        core = lax.rem(lax.axis_index("row"), 2)

        @pl.when(core == 0)
        def _():
            work[0] = x_ref[...]
            work[1] = y_ref[...]

        @pl.when(core == 1)
        def _():
            work[0] = y_ref[...]
            work[1] = x_ref[...]

        u11, m11 = eliminate(work[0, :half, :])
        below = jnp.concatenate([work[0, half:, :], work[1, half:, :]], axis=0)
        l21 = lax.dot_general(below, m11, NT, precision=HIGHEST, preferred_element_type=jnp.float32)
        rest = work[1, :half, :] - lax.dot_general(
            l21, l21, NT, precision=HIGHEST, preferred_element_type=jnp.float32)
        u22, m22 = eliminate(rest)
        m21 = jnp.dot(l21, m11, precision=HIGHEST, preferred_element_type=jnp.float32)
        m21 = -jnp.dot(m22, m21, precision=HIGHEST, preferred_element_type=jnp.float32)
        zero = jnp.zeros((half, half), jnp.float32)
        tri[:half, :half] = u11
        tri[:half, half:] = l21.T
        tri[half:, :half] = zero
        tri[half:, half:] = u22
        low[:half, :half] = m11
        low[:half, half:] = zero
        low[half:, :half] = m21
        low[half:, half:] = m22

    shape = jax.ShapeDtypeStruct((n, n), jnp.float32)
    return pl.pallas_call(kernel, name="factor", in_specs=[VMEM] * 2, out_specs=[VMEM] * 2,
                          scratch_shapes=[pltpu.VMEM((2, rows, half), jnp.float32)],
                          out_shape=[shape] * 2)(own, other)


def basis_call(name, inverse, field, local, shifts, dtype):
    n, width = field.shape
    groups = n // local

    def kernel(inv, f, *outs):
        col = lax.axis_index("col")
        parts = []
        for s in shifts:
            at = pl.multiple_of(lax.rem(col + s, groups) * local, local)
            m = inv[pl.ds(at, local), :]
            high = m.astype(jnp.bfloat16)
            m = m - high.astype(jnp.float32)
            mid = m.astype(jnp.bfloat16)
            m = m - mid.astype(jnp.float32)
            parts += [high, mid, m.astype(jnp.bfloat16)]
        lhs = jnp.concatenate(parts, axis=0)
        step = 256
        for c in range(0, width, step):
            r = jnp.dot(lhs, f[:, c:c + step], preferred_element_type=jnp.float32)
            for i in range(len(shifts)):
                at = 3 * i * local
                v = r[at:at + local] + (r[at + local:at + 2 * local] + r[at + 2 * local:at + 3 * local])
                outs[i][:, c:c + step] = v.astype(dtype)

    shape = jax.ShapeDtypeStruct((local, width), dtype)
    return pl.pallas_call(kernel, name=name, in_specs=[VMEM] * 2, out_specs=[VMEM] * len(shifts),
                          out_shape=[shape] * len(shifts))(inverse, field)


def gather_call(mine, got, inner, outer, block_rows):
    local = mine.shape[0]
    parts = 1 + len(got)

    def kernel(*refs):
        out = refs[-1]
        col = lax.axis_index("col")
        for s in range(parts):
            q = lax.rem(col - s + parts, parts)
            src = refs[s]
            out[:, lanes(W + q * inner, inner)] = src[:, :inner * LANE].astype(jnp.float32)
            edge = jnp.where(q < parts // 2, q * outer, block_rows - (parts - q) * outer)
            out[:, lanes(edge, outer)] = src[:, inner * LANE:].astype(jnp.float32)

    return pl.pallas_call(kernel, name="collect", in_specs=[VMEM] * parts, out_specs=VMEM,
                          out_shape=jax.ShapeDtypeStruct((local, block_rows * LANE), jnp.float32),
                          )(mine, *got)


def on_device(blocks, col_index, live_slots, vectors, center, halfwidth, *, ny, nz):
    block_rows = blocks.shape[0]
    local = vectors.shape[0]
    n_row, n_col = lax.axis_size("row"), lax.axis_size("col")
    order_all = vectors.shape[1] * n_row
    vectors_all = local * n_col
    edge = W * LANE
    inside = block_rows - 2 * W
    inner, outer = inside // n_col, 2 * W // n_col
    scal = jnp.concatenate([center, 1.0 / halfwidth])

    def spot(z, y, c):
        return (z * ny + y) * 2 + c

    every = [(z, y, c) for z in range(nz) for y in range(ny) for c in range(2)]
    swap = [(i, i ^ 1) for i in range(n_row)]

    def along_y(s):
        return [(spot(z, y, c), spot(z, (y + s) % ny, c)) for z, y, c in every]

    def along_z(s):
        return [(spot(z, y, c), spot((z + s) % nz, y, c)) for z, y, c in every]

    def along_x(s):
        return [(i, (i + s) % n_col) for i in range(n_col)]

    def y_of():
        return lax.rem(lax.div(lax.axis_index("row"), 2), ny)

    up = [(i, i + 1) for i in range(n_row - 1)]
    down = [(i + 1, i) for i in range(n_row - 1)]

    def halo(first, last):
        return lax.ppermute(last, "row", up), lax.ppermute(first, "row", down)

    def common(name, second, groups, per_group, row_of, pieces, outs, out_of, plain=None):
        return apply_call(name, second, block_rows, groups, per_group, row_of,
                          [at for _, at in pieces], scal, col_index, live_slots, blocks,
                          [p for p, _ in pieces], plain, outs, out_of, None)

    before, after = halo(vectors[:, :edge], vectors[:, -edge:])
    (mid,) = common("first_inside", False, inside // 8, 8, lambda g: W + 8 * g, [(vectors, W)],
                    [inside], lambda i: (0, 8 * i))
    low, high = common("first_edge", False, 2, W, lambda g: g * (block_rows - W),
                       [(before, 0), (vectors, W), (after, W + block_rows)], [W, W],
                       lambda i: (i, 0))
    before2, after2 = halo(low, high)

    def dest(g):
        return lax.rem(lax.axis_index("col") + g, n_col)

    own = [(low, W), (mid, 2 * W), (high, block_rows)]
    inner_out = common("second_inside", True, n_col, inner, lambda g: W + inner * dest(g), own,
                       [inner] * n_col, lambda i: (i, 0), vectors)

    def edge_row(g):
        q = dest(g)
        return jnp.where(q < n_col // 2, q * outer, block_rows - (n_col - q) * outer)

    inner_got = [lax.ppermute(inner_out[s], "col", along_x(s)) for s in range(1, n_col)]
    outer_out = common("second_edge", True, n_col, outer, edge_row,
                       [(before2, 0), *own, (after2, W + block_rows)], [outer] * n_col,
                       lambda i: (i, 0), vectors)
    outer_got = [lax.ppermute(outer_out[s], "col", along_x(s)) for s in range(1, n_col)]

    field, keep, send = gram_call([inner_out[0], outer_out[0]], [inner_got, outer_got], order_all,
                                  vectors_all)
    other = lax.ppermute(send, "row", swap)
    parts = split_call(keep, other, y_of, ny)
    got = [lax.ppermute(parts[s], "row", along_y(s)) for s in range(1, ny)]

    def total(own_part, got):
        terms = [own_part, *got]
        while len(terms) > 1:
            h = len(terms) // 2
            terms = [terms[i] + terms[i + h] for i in range(h)]
        return terms[0]

    piece = total(parts[0], got)
    piece = total(piece, [lax.ppermute(piece, "col", along_x(s)) for s in range(1, n_col)])
    piece = total(piece, [lax.ppermute(piece, "row", along_z(s)) for s in range(1, nz)])
    mine = merge_call([piece] + [lax.ppermute(piece, "row", along_y(s)) for s in range(1, ny)], y_of)
    triangle, inverse = factor_call(mine, lax.ppermute(mine, "row", swap))

    away = basis_call("basis_away", inverse, field, local, range(1, n_col), jnp.bfloat16)
    back = [lax.ppermute(away[s - 1], "col", along_x(s)) for s in range(1, n_col)]
    (home,) = basis_call("basis_home", inverse, field, local, (0,), jnp.float32)
    return gather_call(home, back, inner, outer, block_rows), triangle


def solution(mesh):
    in_specs = (P("row", None, None, None), P("row", None), P("row"), P("col", "row"), P(), P())
    out_specs = (P("col", "row"), P())
    ny, nz = 4, mesh.shape["row"] // 8

    def body(*args):
        return on_device(*args, ny=ny, nz=nz)

    return jax.shard_map(body, mesh=mesh, in_specs=in_specs, out_specs=out_specs, check_vma=False)
```

```python
import jax
import jax.numpy as jnp
from jax import lax
from jax.experimental import pallas as pl
from jax.experimental.pallas import tpu as pltpu
from jax.sharding import PartitionSpec as P

W = 8
LANE = 128

NT = (((1,), (1,)), ((), ()))
ANY = pl.BlockSpec(memory_space=pl.ANY)
SMEM = pl.BlockSpec(memory_space=pltpu.SMEM)
VMEM = pl.BlockSpec(memory_space=pltpu.VMEM)
HBM = pl.BlockSpec(memory_space=pltpu.HBM)
HIGHEST = lax.Precision.HIGHEST


def vmem(*arrays):
    return [pltpu.with_memory_space_constraint(a, pltpu.VMEM) for a in arrays]


def lanes(block, count=1):
    return pl.ds(pl.multiple_of(block * LANE, LANE), count * LANE)


def row_product(col_ref, live_ref, first_block, ext, blk, row, at_row, zero_block):
    slots = blk.shape[1]
    live = live_ref[row]
    parts = []
    for k in range(slots):
        at = jnp.where(k < live, col_ref[k, row] - first_block, zero_block)
        parts.append(ext[:, lanes(at)])
    picked = jnp.concatenate(parts, axis=1)
    wide = jnp.concatenate([blk[at_row, k] for k in range(slots)], axis=1)
    return lax.dot_general(wide, picked, NT, preferred_element_type=jnp.float32).T


class Row:
    def __init__(self, center, halfwidth, col, live, blk, block_rows=None):
        self.block_rows = block_rows or blk.shape[0]
        self.col, self.live, self.blk = col, live, blk
        self.first = lax.axis_index("row") * self.block_rows - W
        self.shift, self.scale = center[0], 1.0 / halfwidth[0]

    def step(self, field, row, before=None, at_row=None):
        acc = row_product(self.col, self.live, self.first, field, self.blk, row,
                          row if at_row is None else at_row, self.block_rows + 2 * W)
        own = field[:, lanes(row + W)].astype(jnp.float32)
        value = (acc - self.shift * own) * self.scale
        if before is not None:
            value = 2.0 * value - before[:, lanes(row + W)].astype(jnp.float32)
        return value.astype(jnp.bfloat16)


def params(size):
    return pltpu.CompilerParams(vmem_limit_bytes=size << 20)


def ends_call(vectors, edge):
    width, length = vectors.shape

    def kernel(src, low, high, sem):
        copies = [pltpu.make_async_copy(src.at[:, pl.ds(at, edge)], to, sem.at[i])
                  for i, (at, to) in enumerate([(0, low), (length - edge, high)])]
        for copy in copies:
            copy.start()
        for copy in copies:
            copy.wait()

    return pl.pallas_call(
        kernel, name="ends", in_specs=[HBM], out_specs=[VMEM] * 2,
        out_shape=[pltpu.VMEM((width, edge), jnp.bfloat16)] * 2,
        scratch_shapes=[pltpu.SemaphoreType.DMA((2,))], compiler_params=params(4),
    )(pltpu.with_memory_space_constraint(vectors, pltpu.HBM))


def first_call(small, blocks, vectors, before, after):
    block_rows, width = blocks.shape[0], vectors.shape[0]
    total = block_rows + 2 * W
    group, part = 16, 4
    count = block_rows // group

    def kernel(center, halfwidth, col, live, blk_hbm, vec_hbm, before, after, field, field2,
               low, high, blk, sem, bsem):
        load = pltpu.make_async_copy(vec_hbm, field.at[:, pl.ds(W * LANE, block_rows * LANE)], sem)
        load.start()

        def chunk(at, n, i):
            return pltpu.make_async_copy(blk_hbm.at[pl.ds(at, n)], blk.at[pl.ds(at, n)], bsem.at[i])

        chunk(0, part, 0).start()
        chunk(part, group - part, count).start()
        for i in range(1, count):
            chunk(i * group, group, i).start()
        zero = jnp.zeros((width, LANE), jnp.bfloat16)
        field[:, total * LANE:] = zero
        field2[:, total * LANE:] = zero
        field[:, :W * LANE] = before[...]
        field[:, (block_rows + W) * LANE:total * LANE] = after[...]
        rows = Row(center, halfwidth, col, live, blk)
        load.wait()

        def run(at, n):
            for r in range(n):
                field2[:, lanes(at + r + W)] = rows.step(field, at + r)

        def body(g, carry):
            chunk(g * group, group, g).wait()
            run(g * group, group)
            return carry

        chunk(0, part, 0).wait()
        run(0, part)
        chunk(part, group - part, count).wait()
        run(part, group - part)
        lax.fori_loop(1, count, body, 0)
        low[...] = field2[:, W * LANE:2 * W * LANE]
        high[...] = field2[:, block_rows * LANE:(block_rows + W) * LANE]

    kept = pltpu.VMEM((width, (total + 1) * LANE), jnp.bfloat16)
    out = pltpu.VMEM((width, W * LANE), jnp.bfloat16)
    return pl.pallas_call(
        kernel, name="first", in_specs=[SMEM] * 4 + [HBM] * 2 + [VMEM] * 2, out_specs=[VMEM] * 4,
        out_shape=[kept, kept, out, out],
        scratch_shapes=[pltpu.VMEM(blocks.shape, jnp.bfloat16), pltpu.SemaphoreType.DMA,
                        pltpu.SemaphoreType.DMA((count + 1,))],
        compiler_params=params(40),
    )(*small, *[pltpu.with_memory_space_constraint(a, pltpu.HBM) for a in (blocks, vectors)],
      *vmem(before, after))


def second_call(name, small, blocks, field, field2, halo, parts, count, row_of, together=1):
    width = field.shape[0]
    block_rows = blocks.shape[0]
    n_halo = len(halo)
    piece = 4
    pieces = count // piece

    def kernel(*refs):
        center, halfwidth, col, live, blk_hbm, field, field2 = refs[:7]
        outs = refs[7 + n_halo:7 + n_halo + parts]
        blk, bsem, stage, sem = refs[-4:]

        def chunk(g, u):
            return pltpu.make_async_copy(blk_hbm.at[pl.ds(row_of(g) + u * piece, piece)],
                                         blk.at[pl.ds(g * count + u * piece, piece)],
                                         bsem.at[g * pieces + u])

        for g in range(parts):
            for u in range(pieces):
                chunk(g, u).start()
        if n_halo:
            before, after = refs[7:7 + n_halo]
            field2 = refs[7 + n_halo + parts]
            field2[:, :W * LANE] = before[...]
            field2[:, (block_rows + W) * LANE:(block_rows + 2 * W) * LANE] = after[...]
        rows = Row(center, halfwidth, col, live, blk, block_rows)

        def body(t, carry):
            for u in range(together):
                for i in range(pieces):
                    chunk(t * together + u, i).wait()
            for u in range(together):
                g = t * together + u
                at = row_of(g)
                for r in range(count):
                    stage[g, :, r * LANE:(r + 1) * LANE] = rows.step(
                        field2, at + r, field, g * count + r)
            for i in range(parts):
                @pl.when(t == i // together)
                def _(i=i):
                    pltpu.make_async_copy(stage.at[i], outs[i], sem.at[i]).start()
            return carry

        lax.fori_loop(0, parts // together, body, 0)
        for i in range(parts):
            pltpu.make_async_copy(stage.at[i], outs[i], sem.at[i]).wait()

    out_shape = [pltpu.VMEM((width, count * LANE), jnp.bfloat16)] * parts
    out_specs = [VMEM] * parts
    aliases = {}
    if n_halo:
        out_shape.append(pltpu.VMEM(field2.shape, jnp.bfloat16))
        out_specs.append(VMEM)
        aliases = {6: parts}
    return pl.pallas_call(
        kernel, name=name, in_specs=[SMEM] * 4 + [HBM] + [VMEM] * (2 + n_halo),
        out_specs=out_specs, out_shape=out_shape, input_output_aliases=aliases,
        compiler_params=params(32),
        scratch_shapes=[pltpu.VMEM((parts * count, *blocks.shape[1:]), jnp.bfloat16),
                        pltpu.SemaphoreType.DMA((parts * pieces,)),
                        pltpu.VMEM((parts, width, count * LANE), jnp.bfloat16),
                        pltpu.SemaphoreType.DMA((parts,))],
    )(*small, pltpu.with_memory_space_constraint(blocks, pltpu.HBM), field, field2, *halo)[:parts]


def gram_call(mine, got, order_all, vectors_all):
    local, n_pieces = mine[0].shape[0], len(mine)
    widths = [m.shape[1] for m in mine]
    width = sum(widths)
    groups = vectors_all // local
    half = vectors_all // 2
    quarter = half // 2
    arrays = [a for m, g in zip(mine, got) for a in (m, *g)]

    def kernel(*refs):
        srcs = refs[:len(arrays)]
        keep, send, field = refs[len(arrays):]
        col = lax.axis_index("col")
        start = 0
        for p in range(n_pieces):
            for s in range(groups):
                to = lax.rem(col - s + groups, groups) * local
                field[pl.ds(pl.multiple_of(to, local), local), start:start + widths[p]] = (
                    srcs[p * groups + s][...])
            start += widths[p]
        f = field[...]
        g = lax.dot_general(f, f, NT, preferred_element_type=jnp.float32) * (1.0 / order_all)
        core = lax.rem(lax.axis_index("row"), 2)

        def put(low, high):
            low[:half, :] = g[:half, :half]
            low[half:, :] = g[half:half + quarter, :half]
            high[:half, :] = g[half:, half:]
            high[half:, :] = g[half + quarter:, :half]

        @pl.when(core == 0)
        def _():
            put(keep, send)

        @pl.when(core == 1)
        def _():
            put(send, keep)

    packed = pltpu.VMEM((half + quarter, half), jnp.float32)
    return pl.pallas_call(
        kernel, name="gram", in_specs=[VMEM] * len(arrays), out_specs=[VMEM] * 2,
        scratch_shapes=[pltpu.VMEM((vectors_all, width), jnp.bfloat16)],
        out_shape=[packed, packed], compiler_params=params(16),
    )(*vmem(*arrays))


def split_call(keep, other, axis, parts):
    rows = keep.shape[0] // parts

    def kernel(a, b, *outs):
        me = lax.axis_index(axis)
        for s in range(parts):
            at = pl.ds(pl.multiple_of(lax.rem(me + s, parts) * rows, 8), rows)
            outs[s][...] = a[at, :] + b[at, :]

    return pl.pallas_call(kernel, name="split", in_specs=[VMEM] * 2, out_specs=[VMEM] * parts,
                          out_shape=[pltpu.VMEM((rows, keep.shape[1]), jnp.float32)] * parts,
                          compiler_params=params(8))(*vmem(keep, other))


def merge_call(pieces, axis):
    parts, (rows, width) = len(pieces), pieces[0].shape

    def kernel(*refs):
        out = refs[-1]
        me = lax.axis_index(axis)
        for s in range(parts):
            at = pl.ds(pl.multiple_of(lax.rem(me - s + parts, parts) * rows, 8), rows)
            out[at, :] = refs[s][...]

    return pl.pallas_call(kernel, name="merge", in_specs=[VMEM] * parts, out_specs=VMEM,
                          out_shape=pltpu.VMEM((rows * parts, width), jnp.float32),
                          compiler_params=params(8))(*vmem(*pieces))


def eliminate(a):
    n, tile = a.shape[0], 8
    lane = lax.broadcasted_iota(jnp.int32, (tile, n), 1)
    sub = lax.broadcasted_iota(jnp.int32, (tile, n), 0)
    count = n // tile
    panel = range(tile)
    rows = [a[i * tile:(i + 1) * tile, :] for i in range(count)]
    inv = [jnp.where(lane == sub + i * tile, 1.0, 0.0).astype(jnp.float32) for i in range(count)]
    upper, lower = [], []

    def spread(x, r):
        return jnp.broadcast_to(x[r:r + 1, :], (tile, n))

    def column(x, c):
        return jnp.broadcast_to(x[:, c:c + 1], (tile, n))

    def stack(values):
        out = values[0]
        for j in range(1, tile):
            out = jnp.where(sub == j, values[j], out)
        return out

    def add(terms):
        while len(terms) > 1:
            h = len(terms) // 2
            terms = [terms[i] + terms[i + h] for i in range(h)]
        return terms[0]

    for g in range(count):
        c = g * tile
        columns = [column(rows[g], c + j) for j in panel]
        d = {(i, j): spread(columns[j], i) for i in panel for j in range(i + 1)}
        va, vm = [spread(rows[g], j) for j in panel], [spread(inv[g], j) for j in panel]
        t, r = {}, []
        for j in panel:
            r.append(1.0 / d[j, j])
            for i in range(j + 1, tile):
                t[i, j] = d[i, j] * r[j]
                for k in range(j + 1, i + 1):
                    d[i, k] = d[i, k] - t[i, j] * d[k, j]
            for i in range(j + 1, tile):
                va[i], vm[i] = va[i] - t[i, j] * va[j], vm[i] - t[i, j] * vm[j]
        norm = lax.rsqrt(stack([d[j, j] for j in panel]))
        upper.append(jnp.where(lane >= sub + c, stack(va) * norm, 0.0))
        lower.append(stack(vm) * norm)
        if g == count - 1:
            break
        wa, wm = [va[j] * r[j] for j in panel], [vm[j] * r[j] for j in panel]
        for k in range(tile - 1, 0, -1):
            for i in range(k):
                wa[i], wm[i] = wa[i] - t[k, i] * wa[k], wm[i] - t[k, i] * wm[k]
        for i in range(g + 1, count):
            p = [column(rows[i], c + j) for j in panel]
            rows[i] = rows[i] - add([p[j] * wa[j] for j in panel])
            inv[i] = inv[i] - add([p[j] * wm[j] for j in panel])
    return jnp.concatenate(upper, axis=0), jnp.concatenate(lower, axis=0)


def factor_call(own, other):
    rows, half = own.shape
    quarter = half // 2
    n = 2 * half

    def kernel(x_ref, y_ref, tri, low, work):
        core = lax.rem(lax.axis_index("row"), 2)

        @pl.when(core == 0)
        def _():
            work[0] = x_ref[...]
            work[1] = y_ref[...]

        @pl.when(core == 1)
        def _():
            work[0] = y_ref[...]
            work[1] = x_ref[...]

        u11, m11 = eliminate(work[0, :half, :])
        below = jnp.concatenate([work[0, half:, :], work[1, half:, :]], axis=0)
        l21 = lax.dot_general(below, m11, NT, precision=HIGHEST, preferred_element_type=jnp.float32)
        rest = work[1, :half, :] - lax.dot_general(
            l21, l21, NT, precision=HIGHEST, preferred_element_type=jnp.float32)
        u22, m22 = eliminate(rest)
        m21 = jnp.dot(l21, m11, precision=HIGHEST, preferred_element_type=jnp.float32)
        m21 = -jnp.dot(m22, m21, precision=HIGHEST, preferred_element_type=jnp.float32)
        zero = jnp.zeros((half, half), jnp.float32)
        tri[:half, :half] = u11
        tri[:half, half:] = l21.T
        tri[half:, :half] = zero
        tri[half:, half:] = u22
        low[:half, :half] = m11
        low[:half, half:] = zero
        low[half:, :half] = m21
        low[half:, half:] = m22

    return pl.pallas_call(kernel, name="factor", in_specs=[VMEM] * 2, out_specs=[VMEM] * 2,
                          scratch_shapes=[pltpu.VMEM((2, rows, half), jnp.float32)],
                          out_shape=[jax.ShapeDtypeStruct((n, n), jnp.float32),
                                     pltpu.VMEM((n, n), jnp.float32)],
                          compiler_params=params(16))(*vmem(own, other))


def rest_call(inner_out, outer_out):
    parts = len(inner_out)
    local, wide = inner_out[0].shape
    width = wide + outer_out[0].shape[1]
    moves = [(s - 1, i, k) for s in range(1, parts)
             for i, k in enumerate(k for k in range(parts) if k != s)]

    def kernel(*refs):
        inner, outer = refs[:parts], refs[parts:2 * parts]
        outs, sem = refs[2 * parts:-1], refs[-1]
        copies = []
        for n, (o, i, k) in enumerate(moves):
            copies.append(pltpu.make_async_copy(
                inner[k], outs[o].at[:, pl.ds(i * width, wide)], sem.at[2 * n]))
            copies.append(pltpu.make_async_copy(
                outer[k], outs[o].at[:, pl.ds(i * width + wide, width - wide)], sem.at[2 * n + 1]))
        for copy in copies:
            copy.start()
        for copy in copies:
            copy.wait()

    shape = jax.ShapeDtypeStruct((local, (parts - 1) * width), jnp.bfloat16)
    return pl.pallas_call(kernel, name="rest", in_specs=[VMEM] * (2 * parts),
                          out_specs=[ANY] * (parts - 1), out_shape=[shape] * (parts - 1),
                          scratch_shapes=[pltpu.SemaphoreType.DMA((2 * len(moves),))],
                          compiler_params=params(8))(*vmem(*inner_out, *outer_out))


def basis_call(inverse, inner_out, outer_out, inner_got, outer_got, rests, block_rows):
    parts = len(inner_out)
    local, wide = inner_out[0].shape
    tail = outer_out[0].shape[1]
    width = wide + tail
    inner, outer = wide // LANE, tail // LANE
    arrays = [*inner_out, *outer_out, *inner_got, *outer_got, *rests]

    def kernel(*refs):
        inv, refs = refs[0], refs[1:]
        mine_in, mine_out = refs[:parts], refs[parts:2 * parts]
        got_in, got_out = refs[2 * parts:3 * parts - 1], refs[3 * parts - 1:4 * parts - 2]
        rest = refs[4 * parts - 2:5 * parts - 3]
        out, stage, sem = refs[5 * parts - 3:]
        col = lax.axis_index("col")
        m = inv[pl.ds(pl.multiple_of(col * local, local), local), :]
        m = pltpu.roll(m, lax.rem(parts - col, parts) * local, 1)
        high = m.astype(jnp.bfloat16)
        m = m - high.astype(jnp.float32)
        mid = m.astype(jnp.bfloat16)
        m = m - mid.astype(jnp.float32)
        lhs = jnp.concatenate([high, mid, m.astype(jnp.bfloat16)], axis=0)

        def source(j, s, lo, hi):
            k = (j + s) % parts
            if s == 0:
                ref, at = (mine_in[k], lo) if lo < wide else (mine_out[k], lo - wide)
            elif j == 0:
                ref, at = (got_in[s - 1], lo) if lo < wide else (got_out[s - 1], lo - wide)
            else:
                ref, at = rest[s - 1], [i for i in range(parts) if i != s].index(k) * width + lo
            return ref[:, at:at + hi - lo]

        step = 512
        copies = []
        for j in range(parts):
            q = lax.rem(col + j, parts)
            for lo in range(0, width, step):
                rhs = jnp.concatenate(
                    [source(j, (parts - t) % parts, lo, lo + step) for t in range(parts)], axis=0)
                r = jnp.dot(lhs, rhs, preferred_element_type=jnp.float32)
                stage[j, :, lo:lo + step] = r[:local] + (r[local:2 * local] + r[2 * local:])
            edge = jnp.where(q < parts // 2, q * outer, block_rows - (parts - q) * outer)
            for i, (frm, n, to) in enumerate([(0, inner, W + q * inner), (inner, outer, edge)]):
                copy = pltpu.make_async_copy(stage.at[j, :, pl.ds(frm * LANE, n * LANE)],
                                             out.at[:, lanes(to, n)], sem.at[2 * j + i])
                copy.start()
                copies.append(copy)
        for copy in copies:
            copy.wait()

    return pl.pallas_call(
        kernel, name="basis", in_specs=[VMEM] * (1 + len(arrays)), out_specs=ANY,
        out_shape=jax.ShapeDtypeStruct((local, block_rows * LANE), jnp.float32),
        scratch_shapes=[pltpu.VMEM((parts, local, width), jnp.float32),
                        pltpu.SemaphoreType.DMA((2 * parts,))],
        compiler_params=params(16),
    )(*vmem(inverse, *arrays))


def on_device(blocks, col_index, live_slots, vectors, center, halfwidth):
    block_rows = blocks.shape[0]
    local = vectors.shape[0]
    n_row, n_col = lax.axis_size("row"), lax.axis_size("col")
    order_all = vectors.shape[1] * n_row
    vectors_all = local * n_col
    edge = W * LANE
    inside = block_rows - 2 * W
    inner, outer = inside // n_col, 2 * W // n_col

    swap = [(i, i ^ 1) for i in range(n_row)]

    def along_x(s):
        return [(i, (i + s) % n_col) for i in range(n_col)]

    up = [(i, i + 1) for i in range(n_row - 1)]
    down = [(i + 1, i) for i in range(n_row - 1)]

    def halo(first, last):
        return lax.ppermute(last, "row", up), lax.ppermute(first, "row", down)

    small = (center, halfwidth, col_index.T, live_slots)

    before, after = halo(*ends_call(vectors, edge))
    field1, field2, low, high = first_call(small, blocks, vectors, before, after)
    before2, after2 = halo(low, high)

    def dest(g):
        return lax.rem(lax.axis_index("col") + g, n_col)

    inner_out = second_call("second_inside", small, blocks, field1, field2, (), n_col, inner,
                            lambda g: W + inner * dest(g))

    def edge_row(g):
        q = dest(g)
        return jnp.where(q < n_col // 2, q * outer, block_rows - (n_col - q) * outer)

    inner_got = [lax.ppermute(inner_out[s], "col", along_x(s)) for s in range(1, n_col)]
    outer_out = second_call("second_edge", small, blocks, field1, field2, (before2, after2), n_col,
                            outer, edge_row, 2)
    outer_got = [lax.ppermute(outer_out[s], "col", along_x(s)) for s in range(1, n_col)]

    rest_out = rest_call(inner_out, outer_out)
    keep, send = gram_call([inner_out[0], outer_out[0]], [inner_got, outer_got], order_all,
                           vectors_all)
    other = lax.ppermute(send, "row", swap)
    parts = split_call(keep, other, "col", n_col)
    got = [lax.ppermute(parts[s], "col", along_x(s)) for s in range(1, n_col)]
    piece = (parts[0] + got[1]) + (got[0] + got[2])

    *rest_out, piece = lax.optimization_barrier((*rest_out, piece))
    rest_got = [lax.ppermute(rest_out[s - 1], "col", along_x(s)) for s in range(1, n_col)]
    for bit in range(1, n_row.bit_length() - 1):
        piece = piece + lax.ppermute(piece, "row", [(i, i ^ (1 << bit)) for i in range(n_row)])
    mine = merge_call(
        [piece] + [lax.ppermute(piece, "col", along_x(s)) for s in range(1, n_col)], "col")
    triangle, inverse = factor_call(mine, lax.ppermute(mine, "row", swap))
    basis = basis_call(inverse, inner_out, outer_out, inner_got, outer_got, rest_got, block_rows)
    return basis, triangle


def solution(mesh):
    in_specs = (P("row", None, None, None), P("row", None), P("row"), P("col", "row"), P(), P())
    out_specs = (P("col", "row"), P())
    return jax.shard_map(on_device, mesh=mesh, in_specs=in_specs, out_specs=out_specs, check_vma=False)
```

```python
import jax
import jax.numpy as jnp
from jax import lax
from jax.experimental import pallas as pl
from jax.experimental.pallas import tpu as pltpu
from jax.sharding import PartitionSpec as P

W = 8
LANE = 128

NT = (((1,), (1,)), ((), ()))
ANY = pl.BlockSpec(memory_space=pl.ANY)
SMEM = pl.BlockSpec(memory_space=pltpu.SMEM)
VMEM = pl.BlockSpec(memory_space=pltpu.VMEM)
HBM = pl.BlockSpec(memory_space=pltpu.HBM)
HIGHEST = lax.Precision.HIGHEST


def vmem(*arrays):
    return [pltpu.with_memory_space_constraint(a, pltpu.VMEM) for a in arrays]


def lanes(block, count=1):
    return pl.ds(pl.multiple_of(block * LANE, LANE), count * LANE)


def row_product(col_ref, live_ref, first_block, ext, blk, row, at_row, zero_block):
    slots = blk.shape[1]
    live = live_ref[row]
    parts = []
    for k in range(slots):
        at = jnp.where(k < live, col_ref[k, row] - first_block, zero_block)
        parts.append(ext[:, lanes(at)])
    picked = jnp.concatenate(parts, axis=1)
    wide = jnp.concatenate([blk[at_row, k] for k in range(slots)], axis=1)
    return lax.dot_general(wide, picked, NT, preferred_element_type=jnp.float32).T


class Row:
    def __init__(self, center, halfwidth, col, live, blk, block_rows=None):
        self.block_rows = block_rows or blk.shape[0]
        self.col, self.live, self.blk = col, live, blk
        self.first = lax.axis_index("row") * self.block_rows - W
        self.shift, self.scale = center[0], 1.0 / halfwidth[0]

    def step(self, field, row, before=None, at_row=None):
        acc = row_product(self.col, self.live, self.first, field, self.blk, row,
                          row if at_row is None else at_row, self.block_rows + 2 * W)
        own = field[:, lanes(row + W)].astype(jnp.float32)
        value = (acc - self.shift * own) * self.scale
        if before is not None:
            value = 2.0 * value - before[:, lanes(row + W)].astype(jnp.float32)
        return value.astype(jnp.bfloat16)


def params(size):
    return pltpu.CompilerParams(vmem_limit_bytes=size << 20)


def ends_call(vectors, edge):
    width, length = vectors.shape

    def kernel(src, low, high, sem):
        copies = [pltpu.make_async_copy(src.at[:, pl.ds(at, edge)], to, sem.at[i])
                  for i, (at, to) in enumerate([(0, low), (length - edge, high)])]
        for copy in copies:
            copy.start()
        for copy in copies:
            copy.wait()

    return pl.pallas_call(
        kernel, name="ends", in_specs=[HBM], out_specs=[VMEM] * 2,
        out_shape=[pltpu.VMEM((width, edge), jnp.bfloat16)] * 2,
        scratch_shapes=[pltpu.SemaphoreType.DMA((2,))], compiler_params=params(4),
    )(pltpu.with_memory_space_constraint(vectors, pltpu.HBM))


def first_call(small, blocks, vectors, before, after):
    block_rows, width = blocks.shape[0], vectors.shape[0]
    total = block_rows + 2 * W
    group, part = 16, 4
    count = block_rows // group

    def kernel(center, halfwidth, col, live, blk_hbm, vec_hbm, before, after, field, field2,
               low, high, blk, sem, bsem):
        load = pltpu.make_async_copy(vec_hbm, field.at[:, pl.ds(W * LANE, block_rows * LANE)], sem)
        load.start()

        def chunk(at, n, i):
            return pltpu.make_async_copy(blk_hbm.at[pl.ds(at, n)], blk.at[pl.ds(at, n)], bsem.at[i])

        chunk(0, part, 0).start()
        chunk(part, group - part, count).start()
        for i in range(1, count):
            chunk(i * group, group, i).start()
        zero = jnp.zeros((width, LANE), jnp.bfloat16)
        field[:, total * LANE:] = zero
        field2[:, total * LANE:] = zero
        field[:, :W * LANE] = before[...]
        field[:, (block_rows + W) * LANE:total * LANE] = after[...]
        rows = Row(center, halfwidth, col, live, blk)
        load.wait()

        def run(at, n):
            for r in range(n):
                field2[:, lanes(at + r + W)] = rows.step(field, at + r)

        def body(g, carry):
            chunk(g * group, group, g).wait()
            run(g * group, group)
            return carry

        chunk(0, part, 0).wait()
        run(0, part)
        chunk(part, group - part, count).wait()
        run(part, group - part)
        lax.fori_loop(1, count, body, 0)
        low[...] = field2[:, W * LANE:2 * W * LANE]
        high[...] = field2[:, block_rows * LANE:(block_rows + W) * LANE]

    kept = pltpu.VMEM((width, (total + 1) * LANE), jnp.bfloat16)
    out = pltpu.VMEM((width, W * LANE), jnp.bfloat16)
    return pl.pallas_call(
        kernel, name="first", in_specs=[SMEM] * 4 + [HBM] * 2 + [VMEM] * 2, out_specs=[VMEM] * 4,
        out_shape=[kept, kept, out, out],
        scratch_shapes=[pltpu.VMEM(blocks.shape, jnp.bfloat16), pltpu.SemaphoreType.DMA,
                        pltpu.SemaphoreType.DMA((count + 1,))],
        compiler_params=params(40),
    )(*small, *[pltpu.with_memory_space_constraint(a, pltpu.HBM) for a in (blocks, vectors)],
      *vmem(before, after))


def second_call(name, small, blocks, field, field2, halo, parts, count, row_of, together=1):
    width = field.shape[0]
    block_rows = blocks.shape[0]
    n_halo = len(halo)
    piece = 4
    pieces = count // piece

    def kernel(*refs):
        center, halfwidth, col, live, blk_hbm, field, field2 = refs[:7]
        outs = refs[7 + n_halo:7 + n_halo + parts]
        blk, bsem, stage, sem = refs[-4:]

        def chunk(g, u):
            return pltpu.make_async_copy(blk_hbm.at[pl.ds(row_of(g) + u * piece, piece)],
                                         blk.at[pl.ds(g * count + u * piece, piece)],
                                         bsem.at[g * pieces + u])

        for g in range(parts):
            for u in range(pieces):
                chunk(g, u).start()
        if n_halo:
            before, after = refs[7:7 + n_halo]
            field2 = refs[7 + n_halo + parts]
            field2[:, :W * LANE] = before[...]
            field2[:, (block_rows + W) * LANE:(block_rows + 2 * W) * LANE] = after[...]
        rows = Row(center, halfwidth, col, live, blk, block_rows)

        def body(t, carry):
            for u in range(together):
                for i in range(pieces):
                    chunk(t * together + u, i).wait()
            for u in range(together):
                g = t * together + u
                at = row_of(g)
                for r in range(count):
                    stage[g, :, r * LANE:(r + 1) * LANE] = rows.step(
                        field2, at + r, field, g * count + r)
            for i in range(parts):
                @pl.when(t == i // together)
                def _(i=i):
                    pltpu.make_async_copy(stage.at[i], outs[i], sem.at[i]).start()
            return carry

        lax.fori_loop(0, parts // together, body, 0)
        for i in range(parts):
            pltpu.make_async_copy(stage.at[i], outs[i], sem.at[i]).wait()

    out_shape = [pltpu.VMEM((width, count * LANE), jnp.bfloat16)] * parts
    out_specs = [VMEM] * parts
    aliases = {}
    if n_halo:
        out_shape.append(pltpu.VMEM(field2.shape, jnp.bfloat16))
        out_specs.append(VMEM)
        aliases = {6: parts}
    return pl.pallas_call(
        kernel, name=name, in_specs=[SMEM] * 4 + [HBM] + [VMEM] * (2 + n_halo),
        out_specs=out_specs, out_shape=out_shape, input_output_aliases=aliases,
        compiler_params=params(32),
        scratch_shapes=[pltpu.VMEM((parts * count, *blocks.shape[1:]), jnp.bfloat16),
                        pltpu.SemaphoreType.DMA((parts * pieces,)),
                        pltpu.VMEM((parts, width, count * LANE), jnp.bfloat16),
                        pltpu.SemaphoreType.DMA((parts,))],
    )(*small, pltpu.with_memory_space_constraint(blocks, pltpu.HBM), field, field2, *halo)[:parts]


def gram_call(mine, got, order_all, vectors_all):
    local, n_pieces = mine[0].shape[0], len(mine)
    widths = [m.shape[1] for m in mine]
    width = sum(widths)
    groups = vectors_all // local
    half = vectors_all // 2
    quarter = half // 2
    arrays = [a for m, g in zip(mine, got) for a in (m, *g)]

    def kernel(*refs):
        srcs = refs[:len(arrays)]
        keep, send, field = refs[len(arrays):]
        col = lax.axis_index("col")
        start = 0
        for p in range(n_pieces):
            for s in range(groups):
                to = lax.rem(col - s + groups, groups) * local
                field[pl.ds(pl.multiple_of(to, local), local), start:start + widths[p]] = (
                    srcs[p * groups + s][...])
            start += widths[p]
        f = field[...]
        g = lax.dot_general(f, f, NT, preferred_element_type=jnp.float32) * (1.0 / order_all)
        core = lax.rem(lax.axis_index("row"), 2)

        def put(low, high):
            low[:half, :] = g[:half, :half]
            low[half:, :] = g[half:half + quarter, :half]
            high[:half, :] = g[half:, half:]
            high[half:, :] = g[half + quarter:, :half]

        @pl.when(core == 0)
        def _():
            put(keep, send)

        @pl.when(core == 1)
        def _():
            put(send, keep)

    packed = pltpu.VMEM((half + quarter, half), jnp.float32)
    return pl.pallas_call(
        kernel, name="gram", in_specs=[VMEM] * len(arrays), out_specs=[VMEM] * 2,
        scratch_shapes=[pltpu.VMEM((vectors_all, width), jnp.bfloat16)],
        out_shape=[packed, packed], compiler_params=params(16),
    )(*vmem(*arrays))


def split_call(keep, other, axis, parts):
    rows = keep.shape[0] // parts

    def kernel(a, b, *outs):
        me = lax.axis_index(axis)
        for s in range(parts):
            at = pl.ds(pl.multiple_of(lax.rem(me + s, parts) * rows, 8), rows)
            outs[s][...] = a[at, :] + b[at, :]

    return pl.pallas_call(kernel, name="split", in_specs=[VMEM] * 2, out_specs=[VMEM] * parts,
                          out_shape=[pltpu.VMEM((rows, keep.shape[1]), jnp.float32)] * parts,
                          compiler_params=params(8))(*vmem(keep, other))


def merge_call(pieces, axis):
    parts, (rows, width) = len(pieces), pieces[0].shape

    def kernel(*refs):
        out = refs[-1]
        me = lax.axis_index(axis)
        for s in range(parts):
            at = pl.ds(pl.multiple_of(lax.rem(me - s + parts, parts) * rows, 8), rows)
            out[at, :] = refs[s][...]

    return pl.pallas_call(kernel, name="merge", in_specs=[VMEM] * parts, out_specs=VMEM,
                          out_shape=pltpu.VMEM((rows * parts, width), jnp.float32),
                          compiler_params=params(8))(*vmem(*pieces))


def eliminate(a):
    n, tile = a.shape[0], 8
    lane = lax.broadcasted_iota(jnp.int32, (tile, n), 1)
    sub = lax.broadcasted_iota(jnp.int32, (tile, n), 0)
    count = n // tile
    panel = range(tile)
    rows = [a[i * tile:(i + 1) * tile, :] for i in range(count)]
    inv = [jnp.where(lane == sub + i * tile, 1.0, 0.0).astype(jnp.float32) for i in range(count)]
    upper, lower = [], []

    def spread(x, r):
        return jnp.broadcast_to(x[r:r + 1, :], (tile, n))

    def column(x, c):
        return jnp.broadcast_to(x[:, c:c + 1], (tile, n))

    def stack(values):
        out = values[0]
        for j in range(1, tile):
            out = jnp.where(sub == j, values[j], out)
        return out

    def add(terms):
        while len(terms) > 1:
            h = len(terms) // 2
            terms = [terms[i] + terms[i + h] for i in range(h)]
        return terms[0]

    for g in range(count):
        c = g * tile
        columns = [column(rows[g], c + j) for j in panel]
        d = {(i, j): spread(columns[j], i) for i in panel for j in range(i + 1)}
        va, vm = [spread(rows[g], j) for j in panel], [spread(inv[g], j) for j in panel]
        t, r = {}, []
        for j in panel:
            r.append(1.0 / d[j, j])
            for i in range(j + 1, tile):
                t[i, j] = d[i, j] * r[j]
                for k in range(j + 1, i + 1):
                    d[i, k] = d[i, k] - t[i, j] * d[k, j]
            for i in range(j + 1, tile):
                va[i], vm[i] = va[i] - t[i, j] * va[j], vm[i] - t[i, j] * vm[j]
        norm = lax.rsqrt(stack([d[j, j] for j in panel]))
        upper.append(jnp.where(lane >= sub + c, stack(va) * norm, 0.0))
        lower.append(stack(vm) * norm)
        if g == count - 1:
            break
        wa, wm = [va[j] * r[j] for j in panel], [vm[j] * r[j] for j in panel]
        for k in range(tile - 1, 0, -1):
            for i in range(k):
                wa[i], wm[i] = wa[i] - t[k, i] * wa[k], wm[i] - t[k, i] * wm[k]
        for i in range(g + 1, count):
            p = [column(rows[i], c + j) for j in panel]
            rows[i] = rows[i] - add([p[j] * wa[j] for j in panel])
            inv[i] = inv[i] - add([p[j] * wm[j] for j in panel])
    return jnp.concatenate(upper, axis=0), jnp.concatenate(lower, axis=0)


def factor_call(own, other):
    rows, half = own.shape
    quarter = half // 2
    n = 2 * half

    def kernel(x_ref, y_ref, tri, low, work):
        core = lax.rem(lax.axis_index("row"), 2)

        @pl.when(core == 0)
        def _():
            work[0] = x_ref[...]
            work[1] = y_ref[...]

        @pl.when(core == 1)
        def _():
            work[0] = y_ref[...]
            work[1] = x_ref[...]

        u11, m11 = eliminate(work[0, :half, :])
        below = jnp.concatenate([work[0, half:, :], work[1, half:, :]], axis=0)
        l21 = lax.dot_general(below, m11, NT, precision=HIGHEST, preferred_element_type=jnp.float32)
        rest = work[1, :half, :] - lax.dot_general(
            l21, l21, NT, precision=HIGHEST, preferred_element_type=jnp.float32)
        u22, m22 = eliminate(rest)
        m21 = jnp.dot(l21, m11, precision=HIGHEST, preferred_element_type=jnp.float32)
        m21 = -jnp.dot(m22, m21, precision=HIGHEST, preferred_element_type=jnp.float32)
        zero = jnp.zeros((half, half), jnp.float32)
        tri[:half, :half] = u11
        tri[:half, half:] = l21.T
        tri[half:, :half] = zero
        tri[half:, half:] = u22
        low[:half, :half] = m11
        low[:half, half:] = zero
        low[half:, :half] = m21
        low[half:, half:] = m22

    return pl.pallas_call(kernel, name="factor", in_specs=[VMEM] * 2, out_specs=[VMEM] * 2,
                          scratch_shapes=[pltpu.VMEM((2, rows, half), jnp.float32)],
                          out_shape=[jax.ShapeDtypeStruct((n, n), jnp.float32),
                                     pltpu.VMEM((n, n), jnp.float32)],
                          compiler_params=params(16))(*vmem(own, other))


def rest_call(inner_out, outer_out):
    parts = len(inner_out)
    local, wide = inner_out[0].shape
    width = wide + outer_out[0].shape[1]
    moves = [(s - 1, i, k) for s in range(1, parts)
             for i, k in enumerate(k for k in range(parts) if k != s)]

    def kernel(*refs):
        inner, outer = refs[:parts], refs[parts:2 * parts]
        outs, sem = refs[2 * parts:-1], refs[-1]
        copies = []
        for n, (o, i, k) in enumerate(moves):
            copies.append(pltpu.make_async_copy(
                inner[k], outs[o].at[:, pl.ds(i * width, wide)], sem.at[2 * n]))
            copies.append(pltpu.make_async_copy(
                outer[k], outs[o].at[:, pl.ds(i * width + wide, width - wide)], sem.at[2 * n + 1]))
        for copy in copies:
            copy.start()
        for copy in copies:
            copy.wait()

    shape = jax.ShapeDtypeStruct((local, (parts - 1) * width), jnp.bfloat16)
    return pl.pallas_call(kernel, name="rest", in_specs=[VMEM] * (2 * parts),
                          out_specs=[ANY] * (parts - 1), out_shape=[shape] * (parts - 1),
                          scratch_shapes=[pltpu.SemaphoreType.DMA((2 * len(moves),))],
                          compiler_params=params(8))(*vmem(*inner_out, *outer_out))


def basis_call(inverse, inner_out, outer_out, inner_got, outer_got, rests, block_rows):
    parts = len(inner_out)
    local, wide = inner_out[0].shape
    tail = outer_out[0].shape[1]
    width = wide + tail
    inner, outer = wide // LANE, tail // LANE
    arrays = [*inner_out, *outer_out, *inner_got, *outer_got, *rests]

    def kernel(*refs):
        inv, refs = refs[0], refs[1:]
        mine_in, mine_out = refs[:parts], refs[parts:2 * parts]
        got_in, got_out = refs[2 * parts:3 * parts - 1], refs[3 * parts - 1:4 * parts - 2]
        rest = refs[4 * parts - 2:5 * parts - 3]
        out, stage, sem = refs[5 * parts - 3:]
        col = lax.axis_index("col")
        m = inv[pl.ds(pl.multiple_of(col * local, local), local), :]
        m = pltpu.roll(m, lax.rem(parts - col, parts) * local, 1)
        high = m.astype(jnp.bfloat16)
        m = m - high.astype(jnp.float32)
        mid = m.astype(jnp.bfloat16)
        m = m - mid.astype(jnp.float32)
        lhs = jnp.concatenate([high, mid, m.astype(jnp.bfloat16)], axis=0)

        def source(j, s, lo, hi):
            k = (j + s) % parts
            if s == 0:
                ref, at = (mine_in[k], lo) if lo < wide else (mine_out[k], lo - wide)
            elif j == 0:
                ref, at = (got_in[s - 1], lo) if lo < wide else (got_out[s - 1], lo - wide)
            else:
                ref, at = rest[s - 1], [i for i in range(parts) if i != s].index(k) * width + lo
            return ref[:, at:at + hi - lo]

        step = 512
        copies = []
        for j in range(parts):
            q = lax.rem(col + j, parts)
            for lo in range(0, width, step):
                rhs = jnp.concatenate(
                    [source(j, (parts - t) % parts, lo, lo + step) for t in range(parts)], axis=0)
                r = jnp.dot(lhs, rhs, preferred_element_type=jnp.float32)
                stage[j, :, lo:lo + step] = r[:local] + (r[local:2 * local] + r[2 * local:])
            edge = jnp.where(q < parts // 2, q * outer, block_rows - (parts - q) * outer)
            for i, (frm, n, to) in enumerate([(0, inner, W + q * inner), (inner, outer, edge)]):
                copy = pltpu.make_async_copy(stage.at[j, :, pl.ds(frm * LANE, n * LANE)],
                                             out.at[:, lanes(to, n)], sem.at[2 * j + i])
                copy.start()
                copies.append(copy)
        for copy in copies:
            copy.wait()

    return pl.pallas_call(
        kernel, name="basis", in_specs=[VMEM] * (1 + len(arrays)), out_specs=ANY,
        out_shape=jax.ShapeDtypeStruct((local, block_rows * LANE), jnp.float32),
        scratch_shapes=[pltpu.VMEM((parts, local, width), jnp.float32),
                        pltpu.SemaphoreType.DMA((2 * parts,))],
        compiler_params=params(16),
    )(*vmem(inverse, *arrays))


def on_device(blocks, col_index, live_slots, vectors, center, halfwidth):
    block_rows = blocks.shape[0]
    local = vectors.shape[0]
    n_row, n_col = lax.axis_size("row"), lax.axis_size("col")
    order_all = vectors.shape[1] * n_row
    vectors_all = local * n_col
    edge = W * LANE
    inside = block_rows - 2 * W
    inner, outer = inside // n_col, 2 * W // n_col

    swap = [(i, i ^ 1) for i in range(n_row)]

    def along_x(s):
        return [(i, (i + s) % n_col) for i in range(n_col)]

    up = [(i, i + 1) for i in range(n_row - 1)]
    down = [(i + 1, i) for i in range(n_row - 1)]

    def halo(first, last):
        return lax.ppermute(last, "row", up), lax.ppermute(first, "row", down)

    small = (center, halfwidth, col_index.T, live_slots)

    before, after = halo(*ends_call(vectors, edge))
    field1, field2, low, high = first_call(small, blocks, vectors, before, after)
    before2, after2 = halo(low, high)

    def dest(g):
        return lax.rem(lax.axis_index("col") + g, n_col)

    inner_out = second_call("second_inside", small, blocks, field1, field2, (), n_col, inner,
                            lambda g: W + inner * dest(g))

    def edge_row(g):
        q = dest(g)
        return jnp.where(q < n_col // 2, q * outer, block_rows - (n_col - q) * outer)

    inner_got = [lax.ppermute(inner_out[s], "col", along_x(s)) for s in range(1, n_col)]
    outer_out = second_call("second_edge", small, blocks, field1, field2, (before2, after2), n_col,
                            outer, edge_row, 2)
    outer_got = [lax.ppermute(outer_out[s], "col", along_x(s)) for s in range(1, n_col)]

    rest_out = rest_call(inner_out, outer_out)
    keep, send = gram_call([inner_out[0], outer_out[0]], [inner_got, outer_got], order_all,
                           vectors_all)
    other = lax.ppermute(send, "row", swap)
    parts = split_call(keep, other, "col", n_col)
    got = [lax.ppermute(parts[s], "col", along_x(s)) for s in range(1, n_col)]
    piece = (parts[0] + got[1]) + (got[0] + got[2])

    *rest_out, piece = lax.optimization_barrier((*rest_out, piece))
    rest_got = [lax.ppermute(rest_out[s - 1], "col", along_x(s)) for s in range(1, n_col)]
    for mask in (2, 4, 8, 16, 48):
        piece = piece + lax.ppermute(piece, "row", [(i, i ^ mask) for i in range(n_row)])
    mine = merge_call(
        [piece] + [lax.ppermute(piece, "col", along_x(s)) for s in range(1, n_col)], "col")
    triangle, inverse = factor_call(mine, lax.ppermute(mine, "row", swap))
    basis = basis_call(inverse, inner_out, outer_out, inner_got, outer_got, rest_got, block_rows)
    return basis, triangle


def solution(mesh):
    in_specs = (P("row", None, None, None), P("row", None), P("row"), P("col", "row"), P(), P())
    out_specs = (P("col", "row"), P())
    return jax.shard_map(on_device, mesh=mesh, in_specs=in_specs, out_specs=out_specs, check_vma=False)
```
